32 devices in a mesh: dp: 8 (over y, x, core), seq: 4 (over z).
Axes of the slice: x: 2, y: 2, z: 4, core: 2. Of those that a mesh axis runs over, the one named last changes fastest.
Arguments:
- tokens: bfloat16 [8, 8, 64, 3072], P('dp', 'seq'), may hold values from -6 to 6
- frozen_projection: bfloat16 [8, 8, 64, 4608], P('dp', 'seq'), may hold values from -6 to 6
- output_gradient: bfloat16 [8, 8, 64, 1536], P('dp', 'seq'), may hold values from -6 to 6
- adapter_down: bfloat16 [3072, 8], replicated, may hold values from -0.109375 to 0.109375
- adapter_up: bfloat16 [8, 4608], replicated, may hold values from -2 to 2
- query_norm_gain: float32 [128], replicated, may hold values from 0.5 to 1.5
- key_norm_gain: float32 [128], replicated, may hold values from 0.5 to 1.5
- neighbour_mask: int32 [4, 12, 2], replicated, may hold values 0 or 1
Outputs:
- grad_qkv: bfloat16 [8, 8, 64, 4608], P('dp', 'seq')
- lora_down_grad: float32 [3072, 8], P('dp')
- lora_up_grad: float32 [8, 4608], P(None, 'dp')
The draws below stay inside these ranges and needn't reach their ends.
All inputs are finite; a program needn't handle non-finite values.
Results may differ from the reference program's by a relative error of at most 0.0072.
Values may be sent and summed in bfloat16 or wider, within the bound.
A program may use at most 64 MiB of HBM per device.

```python
import jax
import jax.numpy as jnp
from jax import lax

MODEL_DIMENSION = 3072
LOCAL_HEADS = 12
HEAD_WIDTH = 128
ADAPTER_RANK = 8
SPATIAL = 64
FRAMES_DEV = 2
CLIPS = 8
FRAMES = 8
TILES = 4
TOKENS = 4096
N_SEQ = 4


def touch_ends(result, rng, smallest, largest):
    longest = result.shape.index(max(result.shape))
    spots = []
    for shift in (0, 1):
        where = [jax.random.randint(jax.random.fold_in(rng, axis), (), 0, length) for axis, length in enumerate(result.shape)]
        where[longest] = (where[longest] + shift) % result.shape[longest]
        spots.append(tuple(where))
    return result.at[spots[0]].set(smallest).at[spots[1]].set(largest)


def strengthened(drawn, own_key, source, target, blocks, factor):
    owner, partner = [(jnp.arange(drawn.shape[dim]) // (drawn.shape[dim] // blocks)).reshape([-1 if axis == dim else 1 for axis in range(drawn.ndim)]) for dim in (source, target)]
    chosen = jax.random.permutation(own_key, blocks)[partner]
    strong = (owner == chosen) | (owner == (partner + blocks // 2) % blocks)
    return jnp.where(strong, factor * drawn, drawn)


def block_scale(key, extent, split, low, high):
    factor_of = 1.0
    for position, blocks in split:
        steps = jax.random.uniform(jax.random.fold_in(jax.random.fold_in(key, 6), position), (blocks,), jnp.float32, low / len(split), high / len(split))
        factor_of = factor_of * jnp.repeat(jnp.exp(steps), extent[position] // blocks).reshape((-1,) + (1,) * (len(extent) - 1 - position))
    return factor_of


def gaussian(stream_key, extent, deviation, reach, shards=(), kind=jnp.bfloat16):
    drawn = deviation * jax.random.normal(stream_key, extent, jnp.float32)
    if shards:
        drawn = drawn * block_scale(stream_key, extent, shards, -0.22, 0.18)
    return jnp.clip(drawn, -reach, reach).astype(kind)


def gaussian_with(stream_key, extent, scale, reach, pieces, heavy, kind=jnp.bfloat16):
    drawn = scale * jax.random.normal(stream_key, extent, jnp.float32)
    if pieces:
        drawn = drawn * block_scale(stream_key, extent, pieces, -0.22, 0.18)
    return jnp.clip(strengthened(drawn, jax.random.fold_in(stream_key, 3), *heavy), -reach, reach).astype(kind)


def setup_inputs(seed: int = 0) -> dict:
    key_of = jax.random.split(jax.random.key(seed), 9)
    tokens = gaussian_with(key_of[0], (CLIPS, FRAMES, SPATIAL, MODEL_DIMENSION), 1.0, 6.0, ((0, 8), (1, 4)), (0, 3, 8, 2.0))
    frozen_projection = gaussian(key_of[1], (CLIPS, FRAMES, SPATIAL, 3 * LOCAL_HEADS * HEAD_WIDTH), 1.0, 6.0, ((0, 8), (1, 4)))
    output_gradient = gaussian(key_of[2], (CLIPS, FRAMES, SPATIAL, LOCAL_HEADS * HEAD_WIDTH), 1.0, 6.0, ((0, 8), (1, 4)))
    adapter_down = gaussian(key_of[3], (MODEL_DIMENSION, ADAPTER_RANK), MODEL_DIMENSION ** -0.5, 0.109375)
    adapter_up = gaussian(key_of[4], (ADAPTER_RANK, 3 * LOCAL_HEADS * HEAD_WIDTH), ADAPTER_RANK ** -0.5, 2.0)
    query_norm_gain = jnp.clip(1.0 + 0.1 * jax.random.normal(key_of[5], (HEAD_WIDTH,), jnp.float32), 0.5, 1.5)
    key_norm_gain = jnp.clip(1.0 + 0.1 * jax.random.normal(key_of[6], (HEAD_WIDTH,), jnp.float32), 0.5, 1.5)
    neighbour_mask = touch_ends((jax.random.randint(key_of[7], (TILES, LOCAL_HEADS, 2), 0, 4) < 3).astype(jnp.int32), jax.random.fold_in(key_of[7], 1), 0, 1)
    return dict(tokens=tokens, frozen_projection=frozen_projection, output_gradient=output_gradient, adapter_down=adapter_down, adapter_up=adapter_up, query_norm_gain=query_norm_gain, key_norm_gain=key_norm_gain, neighbour_mask=neighbour_mask)


epsilon = 1e-06

def head_norm(values, gain_vector):
    inverse = lax.rsqrt(lax.optimization_barrier(jnp.mean(values * values, axis=-1, keepdims=True)) + epsilon)
    return (values * inverse * gain_vector, inverse)

def head_norm_grad(values, inverse, gain_vector, upstream):
    scaled = upstream * gain_vector
    return inverse * scaled - values * inverse * inverse * inverse * lax.optimization_barrier(jnp.mean(scaled * values, axis=-1, keepdims=True))

def window_mask(block_index, neighbour_mask, query_rows):
    keep_row = lax.dynamic_index_in_dim(neighbour_mask, block_index, 0, keepdims=False).astype(jnp.float32)
    has_below = (block_index > 0).astype(jnp.float32)
    has_above = (block_index < N_SEQ - 1).astype(jnp.float32)
    head_count = keep_row.shape[0]
    slots = jnp.stack([keep_row[:, 0] * has_below, jnp.ones((head_count,), jnp.float32), keep_row[:, 1] * has_above], axis=1)
    return jnp.broadcast_to(slots[:, :, None], (head_count, 3, query_rows)).reshape(head_count, 3 * query_rows)

def attend(queries, upstream, key_bank, value_bank, allowed):
    head_dim = queries.shape[-1]
    score_scale = head_dim ** (-0.5)
    queries_wide = queries.astype(jnp.float32)
    upstream_wide = upstream.astype(jnp.float32)
    keys_wide = key_bank.astype(jnp.float32)
    values_wide = value_bank.astype(jnp.float32)
    scores = jnp.einsum('hqd,hkd->hqk', queries_wide, keys_wide) * score_scale
    raw_weights = jnp.exp(scores) * allowed[:, None, :]
    weights = raw_weights / lax.optimization_barrier(jnp.sum(raw_weights, axis=-1, keepdims=True))
    weights_low = weights.astype(jnp.bfloat16)
    grad_weights = jnp.einsum('hqd,hkd->hqk', upstream_wide, values_wide)
    row_delta = lax.optimization_barrier(jnp.sum(weights * grad_weights, axis=-1, keepdims=True))
    grad_scores = (weights * (grad_weights - row_delta)).astype(jnp.bfloat16)
    grad_queries = jnp.einsum('hqk,hkd->hqd', grad_scores.astype(jnp.float32), keys_wide) * score_scale
    grad_keys = (jnp.einsum('hqk,hqd->hkd', grad_scores.astype(jnp.float32), queries_wide) * score_scale).astype(jnp.bfloat16)
    grad_values = jnp.einsum('hqk,hqd->hkd', weights_low.astype(jnp.float32), upstream_wide).astype(jnp.bfloat16)
    return (grad_queries, grad_keys, grad_values)

def clip_sweep(tokens, frozen_projection, output_gradient, adapter_down, adapter_up, query_norm_gain, key_norm_gain, neighbour_mask):
    frame_count, spatial, model_width = tokens.shape
    combined_width = frozen_projection.shape[-1]
    embed_width = combined_width // 3
    head_dim = query_norm_gain.shape[0]
    head_count = embed_width // head_dim
    head_shape = (frame_count, spatial, head_count, head_dim)
    query_rows = FRAMES_DEV * spatial
    token_matrix = tokens.reshape(-1, model_width)
    reduced_rows = jnp.dot(token_matrix, adapter_down, preferred_element_type=jnp.float32).astype(jnp.bfloat16)
    projected_rows = frozen_projection.reshape(-1, combined_width).astype(jnp.float32) + jnp.dot(reduced_rows, adapter_up, preferred_element_type=jnp.float32)
    query_raw = projected_rows[:, :embed_width].reshape(head_shape)
    key_raw = projected_rows[:, embed_width:2 * embed_width].reshape(head_shape)
    query_normed, query_inverse = head_norm(query_raw, query_norm_gain)
    key_normed, key_inverse = head_norm(key_raw, key_norm_gain)
    query_low = query_normed.astype(jnp.bfloat16)
    key_low = key_normed.astype(jnp.bfloat16)
    value_low = projected_rows[:, 2 * embed_width:].astype(jnp.bfloat16).reshape(head_shape)
    margin = FRAMES_DEV
    padding = ((margin, margin), (0, 0), (0, 0), (0, 0))
    key_padded = jnp.pad(key_low, padding)
    value_padded = jnp.pad(value_low, padding)
    upstream_heads = output_gradient.reshape(head_shape)
    bank_frames = 3 * FRAMES_DEV

    def block_step(accumulated, block_index):
        first_frame = (block_index * FRAMES_DEV).astype(jnp.int32)
        queries = lax.dynamic_slice_in_dim(query_low, first_frame, FRAMES_DEV, 0).reshape(query_rows, head_count, head_dim).transpose(1, 0, 2)
        upstream = lax.dynamic_slice_in_dim(upstream_heads, first_frame, FRAMES_DEV, 0).reshape(query_rows, head_count, head_dim).transpose(1, 0, 2)
        key_bank = lax.dynamic_slice_in_dim(key_padded, first_frame, bank_frames, 0).reshape(3 * query_rows, head_count, head_dim).transpose(1, 0, 2)
        value_bank = lax.dynamic_slice_in_dim(value_padded, first_frame, bank_frames, 0).reshape(3 * query_rows, head_count, head_dim).transpose(1, 0, 2)
        allowed = window_mask(block_index, neighbour_mask, query_rows)
        grad_queries, grad_keys, grad_values = attend(queries, upstream, key_bank, value_bank, allowed)
        bank_grad = jnp.stack([grad_keys, grad_values]).astype(jnp.float32).transpose(0, 2, 1, 3).reshape(2, bank_frames, spatial, head_count, head_dim)
        current = lax.dynamic_slice_in_dim(accumulated, first_frame, bank_frames, 1)
        accumulated = lax.dynamic_update_slice_in_dim(accumulated, current + bank_grad, first_frame, 1)
        return (accumulated, grad_queries.transpose(1, 0, 2))
    start_bank = jnp.zeros((2, frame_count + 2 * margin, spatial, head_count, head_dim), jnp.float32)
    blocks = jnp.arange(N_SEQ, dtype=jnp.int32)
    accumulated, grad_queries = lax.scan(block_step, start_bank, blocks)
    grad_keys = accumulated[0, margin:margin + frame_count]
    grad_values = accumulated[1, margin:margin + frame_count]
    grad_query_raw = head_norm_grad(query_raw, query_inverse, query_norm_gain, grad_queries.reshape(head_shape))
    grad_key_raw = head_norm_grad(key_raw, key_inverse, key_norm_gain, grad_keys)
    grad_qkv = jnp.concatenate([grad_query_raw.reshape(frame_count, spatial, embed_width), grad_key_raw.reshape(frame_count, spatial, embed_width), grad_values.reshape(frame_count, spatial, embed_width)], axis=-1).astype(jnp.bfloat16)
    gradient_rows = grad_qkv.reshape(-1, combined_width)
    gradient_reduced = lax.dot_general(gradient_rows, adapter_up, (((1,), (1,)), ((), ())), preferred_element_type=jnp.float32).astype(jnp.bfloat16)
    term_up = lax.dot_general(reduced_rows, gradient_rows, (((0,), (0,)), ((), ())), preferred_element_type=jnp.float32)
    term_down = lax.dot_general(token_matrix, gradient_reduced, (((0,), (0,)), ((), ())), preferred_element_type=jnp.float32)
    return (grad_qkv, term_down, term_up)

def reference(tokens, frozen_projection, output_gradient, adapter_down, adapter_up, query_norm_gain, key_norm_gain, neighbour_mask):

    def one_clip(array_list):
        return clip_sweep(array_list[0], array_list[1], array_list[2], adapter_down, adapter_up, query_norm_gain, key_norm_gain, neighbour_mask)
    grad_qkv, terms_down, terms_up = lax.map(one_clip, (tokens, frozen_projection, output_gradient))
    norm_factor = TOKENS ** (-0.5)
    return (grad_qkv, lax.optimization_barrier(jnp.sum(terms_down, axis=0)) * norm_factor, lax.optimization_barrier(jnp.sum(terms_up, axis=0)) * norm_factor)
```

```python
import functools

import jax
import jax.numpy as jnp
from jax import lax
from jax.experimental import pallas as pl
from jax.experimental.pallas import tpu as pltpu
from jax.sharding import PartitionSpec as P

EPSILON = 1e-06
CHUNKS = (2, 2, 2, 2, 2, 2)
F32 = jnp.float32
BF16 = jnp.bfloat16


def dot_nt(a, b):
    return lax.dot_general(a, b, (((1,), (1,)), ((), ())), preferred_element_type=F32)


def dot_nn(a, b):
    return lax.dot_general(a, b, (((1,), (0,)), ((), ())), preferred_element_type=F32)


def dot_tn(a, b):
    return lax.dot_general(a, b, (((0,), (0,)), ((), ())), preferred_element_type=F32)


def kernel(
    geometry,
    tokens_hbm,
    frozen_hbm,
    upstream_hbm,
    down_ref,
    up_ref,
    query_gain_ref,
    key_gain_ref,
    mask_ref,
    grad_hbm,
    lora_down_ref,
    lora_up_ref,
    tokens_ref,
    frozen_ref,
    load_sem,
    query_all,
    upstream_all,
    key_own,
    value_own,
    raw_ref,
    exp_all,
    product_all,
    part_out,
    part_in,
    part_own,
    stat_out,
    stat_in,
    dq_out,
    dq_in,
    dq_own,
    grad_ref,
    term_up,
    low_grad,
    bulk_send,
    bulk_recv,
    stat_send,
    stat_recv,
    dq_send,
    dq_recv,
    store_sem,
    *reduce_refs,
):
    rows, width, head_dim, dp, seq, fused = geometry
    scale = head_dim ** (-0.5)
    heads = width // head_dim
    me = lax.axis_index("seq")
    has_below = me > 0
    has_above = me < seq - 1
    edges = (has_above, has_below)
    sources = (has_below, has_above)
    targets = ({"seq": me + 1}, {"seq": me - 1})
    mesh_id = pl.DeviceIdType.MESH
    barrier = pltpu.get_barrier_semaphore()
    if fused:
        dp_me = lax.axis_index("dp")
        for j in range(1, dp):
            pl.semaphore_signal(
                barrier, inc=1, device_id={"dp": lax.rem(dp_me + j, dp)}, device_id_type=mesh_id
            )
        for j in range(1, seq):
            pl.semaphore_signal(
                barrier, inc=1, device_id={"seq": lax.rem(me + j, seq)}, device_id_type=mesh_id
            )
    else:
        for way in (0, 1):

            @pl.when(edges[way])
            def _():
                pl.semaphore_signal(
                    barrier, inc=1, device_id=targets[way], device_id_type=mesh_id
                )

    load_tokens = pltpu.make_async_copy(tokens_hbm, tokens_ref, load_sem.at[0])
    load_frozen = pltpu.make_async_copy(frozen_hbm, frozen_ref, load_sem.at[1])
    load_upstream = pltpu.make_async_copy(upstream_hbm, upstream_all.at[1], load_sem.at[2])
    load_tokens.start()
    load_frozen.start()
    load_upstream.start()

    for side in (0, 1):

        @pl.when(jnp.logical_not(sources[side]))
        def _():
            query_all[2 * side] = jnp.zeros((rows, width), BF16)
            upstream_all[2 * side] = jnp.zeros((rows, width), BF16)
            part_in[side] = jnp.zeros(part_in.shape[1:], F32)
            stat_in[side] = jnp.zeros(stat_in.shape[1:], F32)
            dq_in[side] = jnp.zeros((rows, width), BF16)

    part_out[...] = jnp.zeros(part_out.shape, F32)
    part_own[...] = jnp.zeros(part_own.shape, F32)
    stat_out[...] = jnp.zeros(stat_out.shape, F32)

    bounds = []
    first = 0
    for count in CHUNKS:
        bounds.append((first, count))
        first += count
    steps = len(bounds)

    def columns(c):
        return pl.ds(bounds[c][0] * head_dim, bounds[c][1] * head_dim)

    def remote(source, target, send, recv, way):
        return pltpu.make_async_remote_copy(
            src_ref=source,
            dst_ref=target,
            send_sem=send,
            recv_sem=recv,
            device_id=targets[way],
            device_id_type=mesh_id,
        )

    def query_copy(c, way):
        return remote(
            query_all.at[1, :, columns(c)],
            query_all.at[2 * way, :, columns(c)],
            bulk_send.at[0, way, c],
            bulk_recv.at[0, way, c],
            way,
        )

    def upstream_copy(c, way):
        return remote(
            upstream_hbm.at[:, columns(c)],
            upstream_all.at[2 * way, :, columns(c)],
            bulk_send.at[1, way, c],
            bulk_recv.at[1, way, c],
            way,
        )

    def part_copy(c, way):
        return remote(
            part_out.at[way, c],
            part_in.at[way, c],
            stat_send.at[0, way, c],
            stat_recv.at[0, way, c],
            way,
        )

    def stat_copy(c, way):
        return remote(
            stat_out.at[c],
            stat_in.at[way, c],
            stat_send.at[1, way, c],
            stat_recv.at[1, way, c],
            way,
        )

    def dq_copy(c, way):
        return remote(
            dq_out.at[way, :, columns(c)],
            dq_in.at[way, :, columns(c)],
            dq_send.at[way, c],
            dq_recv.at[way, c],
            way,
        )

    def launch(copies, c):
        for way in (0, 1):

            @pl.when(edges[way])
            def _():
                for copy in copies:
                    copy(c, way).start()

    def arrive(copies, c):
        for way in (0, 1):

            @pl.when(sources[way])
            def _():
                for copy in copies:
                    copy(c, way).wait_recv()

    def sent(copies, c):
        for way in (0, 1):

            @pl.when(edges[way])
            def _():
                for copy in copies:
                    copy(c, way).wait_send()

    if fused:
        pl.semaphore_wait(barrier, dp + seq - 2)
    else:
        for side in (0, 1):

            @pl.when(sources[side])
            def _():
                pl.semaphore_wait(barrier, 1)

    launch((upstream_copy,), 0)
    launch((upstream_copy,), 1)

    load_tokens.wait()
    low = dot_nt(tokens_ref[...], down_ref[...]).astype(BF16)
    low_t = dot_nt(down_ref[...], tokens_ref[...]).astype(BF16)
    load_frozen.wait()
    query_gain = query_gain_ref[...]
    key_gain = key_gain_ref[...]

    def normed(raw):
        inverse = lax.rsqrt(jnp.mean(raw * raw, axis=-1, keepdims=True) + EPSILON)
        return raw * inverse, inverse

    def project(part, c):
        cut = pl.ds(part * width + bounds[c][0] * head_dim, bounds[c][1] * head_dim)
        return frozen_ref[:, cut].astype(F32) + dot_nn(low, up_ref[:, cut])

    def project_heads(part, c, gain, target):
        raw = project(part, c)
        raw_ref[part, :, columns(c)] = raw
        for i in range(bounds[c][1]):
            h = bounds[c][0] + i
            one = raw[:, i * head_dim : (i + 1) * head_dim]
            target(h, (normed(one)[0] * gain).astype(BF16))

    def put_query(h, value):
        query_all[1, :, pl.ds(h * head_dim, head_dim)] = value

    def put_key(h, value):
        key_own[:, pl.ds(h * head_dim, head_dim)] = value

    for c in range(steps):
        project_heads(0, c, query_gain, put_query)
        if c == 1:
            launch((query_copy,), 0)
            launch((query_copy,), 1)
    for c in range(steps):
        project_heads(1, c, key_gain, put_key)
        value_own[:, columns(c)] = project(2, c).astype(BF16)
    load_upstream.wait()

    slot_tiles = rows

    def spread(below, own, above):
        return jnp.concatenate([below, own, above], axis=1)

    def head_cut(h):
        return pl.ds(h * head_dim, head_dim)

    def stage_scores(c):
        head, count = bounds[c]
        for i in range(count):
            h = head + i
            queries = query_all[:, :, head_cut(h)].reshape(3 * rows, head_dim)
            upstream = upstream_all[:, :, head_cut(h)].reshape(3 * rows, head_dim)
            keep_below = mask_ref[jnp.maximum(me - 1, 0), h, 1].astype(F32)
            keep_above = mask_ref[jnp.minimum(me + 1, seq - 1), h, 0].astype(F32)
            keep_below = keep_below * has_below.astype(F32)
            keep_above = keep_above * has_above.astype(F32)
            keep = spread(
                jnp.full((1, rows), keep_below, F32),
                jnp.ones((1, rows), F32),
                jnp.full((1, rows), keep_above, F32),
            )
            scores = dot_nt(key_own[:, head_cut(h)], queries) * scale
            grown = jnp.exp(scores) * keep
            product = dot_nt(value_own[:, head_cut(h)], upstream)
            exp_all[h] = grown
            product_all[h] = product
            total = jnp.sum(grown, axis=0, keepdims=True)
            moment = jnp.sum(grown * product, axis=0, keepdims=True)
            for row, line in ((i, total), (4 + i, moment)):
                part_out[1, c, pl.ds(row, 1), :] = line[:, :rows]
                part_own[c, pl.ds(row, 1), :] = line[:, rows : 2 * rows]
                part_out[0, c, pl.ds(row, 1), :] = line[:, 2 * rows :]

    def stage_stats(c):
        whole = part_own[c] + part_in[0, c] + part_in[1, c]
        count = bounds[c][1]
        inverse = 1.0 / whole[:count]
        delta = whole[4 : 4 + count] * inverse
        stat_out[c, pl.ds(0, count), :] = inverse
        stat_out[c, pl.ds(4, count), :] = delta

    def norm_grad(raw, gain, upstream):
        unit, inverse = normed(raw)
        scaled = upstream * gain
        return inverse * (scaled - unit * jnp.mean(scaled * unit, axis=-1, keepdims=True))

    def absorb(part, c):
        cut = pl.ds(part * width + bounds[c][0] * head_dim, bounds[c][1] * head_dim)
        grad = grad_ref[:, cut]
        term_up[:, cut] = dot_nn(low_t, grad)
        return dot_nt(up_ref[:, cut], grad)

    def stage_grads(c):
        head, count = bounds[c]
        for i in range(count):
            h = head + i
            queries = query_all[:, :, head_cut(h)].reshape(3 * rows, head_dim)
            upstream = upstream_all[:, :, head_cut(h)].reshape(3 * rows, head_dim)
            inverse = spread(*(ref[c, pl.ds(i, 1), :] for ref in (stat_in.at[0], stat_out, stat_in.at[1])))
            delta = spread(*(ref[c, pl.ds(4 + i, 1), :] for ref in (stat_in.at[0], stat_out, stat_in.at[1])))
            weights = exp_all[h] * inverse
            grad_scores = (weights * (product_all[h] - delta)).astype(BF16)
            grad_query = dot_tn(grad_scores, key_own[:, head_cut(h)]) * scale
            dq_out[1, :, head_cut(h)] = grad_query[:rows].astype(BF16)
            dq_own[:, head_cut(h)] = grad_query[rows : 2 * rows]
            dq_out[0, :, head_cut(h)] = grad_query[2 * rows :].astype(BF16)
        launch((dq_copy,), c)
        for i in range(count):
            h = head + i
            queries = query_all[:, :, head_cut(h)].reshape(3 * rows, head_dim)
            upstream = upstream_all[:, :, head_cut(h)].reshape(3 * rows, head_dim)
            inverse = spread(*(ref[c, pl.ds(i, 1), :] for ref in (stat_in.at[0], stat_out, stat_in.at[1])))
            delta = spread(*(ref[c, pl.ds(4 + i, 1), :] for ref in (stat_in.at[0], stat_out, stat_in.at[1])))
            weights = exp_all[h] * inverse
            grad_scores = (weights * (product_all[h] - delta)).astype(BF16)
            grad_key = dot_nn(grad_scores, queries) * scale
            grad_value = dot_nn(weights.astype(BF16), upstream)
            grad_ref[:, pl.ds(width + h * head_dim, head_dim)] = norm_grad(
                raw_ref[1, :, head_cut(h)], key_gain, grad_key
            ).astype(BF16)
            grad_ref[:, pl.ds(2 * width + h * head_dim, head_dim)] = grad_value.astype(BF16)
        low_grad[...] += absorb(1, c) + absorb(2, c)

    def stage_queries(c):
        head, count = bounds[c]
        for i in range(count):
            h = head + i
            grad_query = (
                dq_own[:, head_cut(h)]
                + dq_in[0, :, head_cut(h)].astype(F32)
                + dq_in[1, :, head_cut(h)].astype(F32)
            )
            grad_ref[:, head_cut(h)] = norm_grad(
                raw_ref[0, :, head_cut(h)], query_gain, grad_query
            ).astype(BF16)
        low_grad[...] += absorb(0, c)

    low_grad[...] = jnp.zeros(low_grad.shape, F32)
    for step in range(steps + 3):
        if step < steps:
            arrive((upstream_copy, query_copy), step)
            stage_scores(step)
            launch((part_copy,), step)
        if 0 <= step - 1 < steps:
            arrive((part_copy,), step - 1)
            stage_stats(step - 1)
            launch((stat_copy,), step - 1)
        if step + 2 < steps:
            launch((upstream_copy, query_copy), step + 2)
        if 0 <= step - 2 < steps:
            arrive((stat_copy,), step - 2)
            stage_grads(step - 2)
        if 0 <= step - 3 < steps:
            arrive((dq_copy,), step - 3)
            stage_queries(step - 3)

    store = pltpu.make_async_copy(grad_ref, grad_hbm, store_sem)
    store.start()
    model_width = tokens_ref.shape[1]
    term_down = dot_nn(low_grad[...].astype(BF16), tokens_ref[...])
    norm_factor = float(dp * seq * rows) ** (-0.5)
    if not fused:
        lora_down_ref[...] = term_down
        lora_up_ref[...] = term_up[...]
    else:
        msg_own, msg_out, msg_in, line_out, line_in, dp_send, dp_recv, seq_send, seq_recv = reduce_refs
        down_share = model_width // dp
        up_share = 3 * width // dp
        packed = msg_own.shape[2]
        filler = 2 * packed - down_share - up_share
        for d in range(dp):
            pieces = [
                term_down[:, d * down_share : (d + 1) * down_share],
                term_up[:, d * up_share : (d + 1) * up_share],
            ]
            if filler:
                pieces.append(jnp.zeros((pieces[0].shape[0], filler), F32))
            line = jnp.concatenate(pieces, axis=1)
            line = jnp.concatenate([line[:, :packed], line[:, packed:]], axis=0)
            msg_own[d] = line
            msg_out[d] = line.astype(BF16)

        def dp_copy(j):
            peer = lax.rem(dp_me + j, dp)
            return pltpu.make_async_remote_copy(
                src_ref=msg_out.at[peer],
                dst_ref=msg_in.at[j - 1],
                send_sem=dp_send.at[j - 1],
                recv_sem=dp_recv.at[j - 1],
                device_id={"dp": peer},
                device_id_type=mesh_id,
            )

        def seq_copy(j):
            peer = lax.rem(me + j, seq)
            return pltpu.make_async_remote_copy(
                src_ref=line_out,
                dst_ref=line_in.at[me],
                send_sem=seq_send.at[j - 1],
                recv_sem=seq_recv.at[j - 1],
                device_id={"seq": peer},
                device_id_type=mesh_id,
            )

        for j in range(1, dp):
            dp_copy(j).start()
        for c in range(steps):
            sent((upstream_copy, query_copy, part_copy, stat_copy, dq_copy), c)
        summed = msg_own[dp_me]
        for j in range(1, dp):
            dp_copy(j).wait_recv()
            summed = summed + msg_in[j - 1].astype(F32)
        line_out[...] = summed.astype(BF16)
        line_in[me] = summed.astype(BF16)
        for j in range(1, seq):
            seq_copy(j).start()
        for j in range(1, dp):
            dp_copy(j).wait_send()
        for j in range(1, seq):
            seq_copy(j).wait_recv()
        result = line_in[0].astype(F32)
        for j in range(1, seq):
            result = result + line_in[j].astype(F32)
        result = result * norm_factor
        half = result.shape[0] // 2
        line = jnp.concatenate([result[:half], result[half:]], axis=1)
        lora_down_ref[...] = line[:, :down_share]
        lora_up_ref[...] = line[:, down_share : down_share + up_share]
        for j in range(1, seq):
            seq_copy(j).wait_send()
    if not fused:
        for c in range(steps):
            sent((upstream_copy, query_copy, part_copy, stat_copy, dq_copy), c)
    store.wait()


def on_device(
    dp,
    seq,
    tokens,
    frozen_projection,
    output_gradient,
    adapter_down,
    adapter_up,
    query_norm_gain,
    key_norm_gain,
    neighbour_mask,
):
    clip_count, frames_dev, spatial, model_width = tokens.shape
    combined = frozen_projection.shape[-1]
    width = combined // 3
    head_dim = query_norm_gain.shape[0]
    heads = width // head_dim
    rank = adapter_up.shape[0]
    rows = clip_count * frames_dev * spatial
    assert clip_count == 1 and sum(CHUNKS) == heads
    steps = len(CHUNKS)
    down_share = model_width // dp
    up_share = combined // dp
    fused = dp <= 8 and seq <= 4 and down_share % 128 == 0
    vmem = pl.BlockSpec(memory_space=pltpu.VMEM)
    anywhere = pl.BlockSpec(memory_space=pl.ANY)
    dma = pltpu.SemaphoreType.DMA
    scratch = [
        pltpu.VMEM((rows, model_width), BF16),
        pltpu.VMEM((rows, combined), BF16),
        dma((3,)),
        pltpu.VMEM((3, rows, width), BF16),
        pltpu.VMEM((3, rows, width), BF16),
        pltpu.VMEM((rows, width), BF16),
        pltpu.VMEM((rows, width), BF16),
        pltpu.VMEM((2, rows, width), F32),
        pltpu.VMEM((heads, rows, 3 * rows), F32),
        pltpu.VMEM((heads, rows, 3 * rows), F32),
        pltpu.VMEM((2, steps, 8, rows), F32),
        pltpu.VMEM((2, steps, 8, rows), F32),
        pltpu.VMEM((steps, 8, rows), F32),
        pltpu.VMEM((steps, 8, rows), F32),
        pltpu.VMEM((2, steps, 8, rows), F32),
        pltpu.VMEM((2, rows, width), BF16),
        pltpu.VMEM((2, rows, width), BF16),
        pltpu.VMEM((rows, width), F32),
        pltpu.VMEM((rows, combined), BF16),
        pltpu.VMEM((rank, combined), F32),
        pltpu.VMEM((rank, rows), F32),
        dma((2, 2, steps)),
        dma((2, 2, steps)),
        dma((2, 2, steps)),
        dma((2, 2, steps)),
        dma((2, steps)),
        dma((2, steps)),
        dma,
    ]
    if fused:
        packed = -(-(down_share + up_share) // 256) * 128
        scratch += [
            pltpu.VMEM((dp, 2 * rank, packed), F32),
            pltpu.VMEM((dp, 2 * rank, packed), BF16),
            pltpu.VMEM((dp - 1, 2 * rank, packed), BF16),
            pltpu.VMEM((2 * rank, packed), BF16),
            pltpu.VMEM((seq, 2 * rank, packed), BF16),
            dma((dp - 1,)),
            dma((dp - 1,)),
            dma((seq - 1,)),
            dma((seq - 1,)),
        ]
        lora_shapes = ((rank, down_share), (rank, up_share))
    else:
        lora_shapes = ((rank, model_width), (rank, combined))
    geometry = (rows, width, head_dim, dp, seq, fused)
    grad, lora_down, lora_up = pl.pallas_call(
        functools.partial(kernel, geometry),
        out_shape=(
            jax.ShapeDtypeStruct((rows, combined), BF16),
            jax.ShapeDtypeStruct(lora_shapes[0], F32),
            jax.ShapeDtypeStruct(lora_shapes[1], F32),
        ),
        in_specs=[anywhere] * 3 + [vmem] * 4 + [pl.BlockSpec(memory_space=pltpu.SMEM)],
        out_specs=(anywhere, vmem, vmem),
        scratch_shapes=scratch,
        compiler_params=pltpu.CompilerParams(
            collective_id=0, has_side_effects=True, vmem_limit_bytes=48 * 1024 * 1024
        ),
        name="tile_attention",
    )(
        tokens.reshape(rows, model_width),
        frozen_projection.reshape(rows, combined),
        output_gradient.reshape(rows, width),
        adapter_down.T,
        adapter_up,
        query_norm_gain.reshape(1, head_dim),
        key_norm_gain.reshape(1, head_dim),
        neighbour_mask,
    )
    grad = grad.reshape(frozen_projection.shape)
    if fused:
        return grad, lora_down.T, lora_up
    norm_factor = float(dp * seq * rows) ** (-0.5)
    whole_down, whole_up = lax.psum((lora_down, lora_up), ("dp", "seq"))
    dp_index = lax.axis_index("dp")
    mine_down = lax.dynamic_slice_in_dim(whole_down, dp_index * down_share, down_share, 1)
    mine_up = lax.dynamic_slice_in_dim(whole_up, dp_index * up_share, up_share, 1)
    return grad, mine_down.T * norm_factor, mine_up * norm_factor


def solution(mesh):
    dp, seq = mesh.shape["dp"], mesh.shape["seq"]
    return jax.shard_map(
        functools.partial(on_device, dp, seq),
        mesh=mesh,
        in_specs=(
            P("dp", "seq", None, None),
            P("dp", "seq", None, None),
            P("dp", "seq", None, None),
            P(),
            P(),
            P(),
            P(),
            P(),
        ),
        out_specs=(P("dp", "seq", None, None), P("dp", None), P(None, "dp")),
        check_vma=False,
    )
```

```python
import functools

import jax
import jax.numpy as jnp
from jax import lax
from jax.experimental import pallas as pl
from jax.experimental.pallas import tpu as pltpu
from jax.sharding import PartitionSpec as P

EPSILON = 1e-06
CHUNKS = (2, 2, 2, 2, 2, 2)
LEAD = 2
F32 = jnp.float32
BF16 = jnp.bfloat16


def dot_nt(a, b):
    return lax.dot_general(a, b, (((1,), (1,)), ((), ())), preferred_element_type=F32)


def dot_nn(a, b):
    return lax.dot_general(a, b, (((1,), (0,)), ((), ())), preferred_element_type=F32)


def dot_tn(a, b):
    return lax.dot_general(a, b, (((0,), (0,)), ((), ())), preferred_element_type=F32)


def kernel(
    geometry,
    tokens_hbm,
    frozen_hbm,
    upstream_hbm,
    down_hbm,
    up_hbm,
    query_gain_hbm,
    key_gain_hbm,
    mask_hbm,
    grad_ref,
    lora_down_ref,
    lora_up_ref,
    tokens_ref,
    frozen_ref,
    down_ref,
    up_ref,
    query_gain_ref,
    key_gain_ref,
    mask_ref,
    load_sem,
    query_all,
    upstream_all,
    key_own,
    value_own,
    raw_ref,
    exp_all,
    product_all,
    part_out,
    part_in,
    part_own,
    stat_out,
    stat_in,
    dq_out,
    dq_in,
    dq_own,
    term_up,
    low_grad,
    bulk_send,
    bulk_recv,
    stat_send,
    stat_recv,
    dq_send,
    dq_recv,
    *reduce_refs,
):
    rows, width, head_dim, dp, seq, fused = geometry
    scale = head_dim ** (-0.5)
    heads = width // head_dim
    me = lax.axis_index("seq")
    has_below = me > 0
    has_above = me < seq - 1
    edges = (has_above, has_below)
    sources = (has_below, has_above)
    targets = ({"seq": me + 1}, {"seq": me - 1})
    mesh_id = pl.DeviceIdType.MESH
    barrier = pltpu.get_barrier_semaphore()
    if fused:
        dp_me = lax.axis_index("dp")
        for j in range(1, dp):
            pl.semaphore_signal(
                barrier, inc=1, device_id={"dp": lax.rem(dp_me + j, dp)}, device_id_type=mesh_id
            )
        for j in range(1, seq):
            pl.semaphore_signal(
                barrier, inc=1, device_id={"seq": lax.rem(me + j, seq)}, device_id_type=mesh_id
            )
    else:
        for way in (0, 1):

            @pl.when(edges[way])
            def _():
                pl.semaphore_signal(
                    barrier, inc=1, device_id=targets[way], device_id_type=mesh_id
                )

    load_tokens = pltpu.make_async_copy(tokens_hbm, tokens_ref, load_sem.at[0])
    load_frozen = pltpu.make_async_copy(frozen_hbm, frozen_ref, load_sem.at[1])
    load_upstream = pltpu.make_async_copy(upstream_hbm, upstream_all.at[1], load_sem.at[2])
    load_small = [
        pltpu.make_async_copy(source, target, load_sem.at[3 + i])
        for i, (source, target) in enumerate(
            (
                (down_hbm, down_ref),
                (up_hbm, up_ref),
                (query_gain_hbm, query_gain_ref),
                (key_gain_hbm, key_gain_ref),
                (mask_hbm, mask_ref),
            )
        )
    ]
    load_tokens.start()
    for load in load_small:
        load.start()
    load_frozen.start()
    load_upstream.start()

    for side in (0, 1):

        @pl.when(jnp.logical_not(sources[side]))
        def _():
            query_all[2 * side] = jnp.zeros((rows, width), BF16)
            upstream_all[2 * side] = jnp.zeros((rows, width), BF16)
            part_in[side] = jnp.zeros(part_in.shape[1:], F32)
            stat_in[side] = jnp.zeros(stat_in.shape[1:], F32)
            dq_in[side] = jnp.zeros((rows, width), BF16)

    part_out[...] = jnp.zeros(part_out.shape, F32)
    part_own[...] = jnp.zeros(part_own.shape, F32)
    stat_out[...] = jnp.zeros(stat_out.shape, F32)

    bounds = []
    first = 0
    for count in CHUNKS:
        bounds.append((first, count))
        first += count
    steps = len(bounds)

    def columns(c):
        return pl.ds(bounds[c][0] * head_dim, bounds[c][1] * head_dim)

    def remote(source, target, send, recv, way):
        return pltpu.make_async_remote_copy(
            src_ref=source,
            dst_ref=target,
            send_sem=send,
            recv_sem=recv,
            device_id=targets[way],
            device_id_type=mesh_id,
        )

    def query_copy(c, way):
        return remote(
            query_all.at[1, :, columns(c)],
            query_all.at[2 * way, :, columns(c)],
            bulk_send.at[0, way, c],
            bulk_recv.at[0, way, c],
            way,
        )

    def upstream_copy(c, way):
        return remote(
            upstream_hbm.at[:, columns(c)],
            upstream_all.at[2 * way, :, columns(c)],
            bulk_send.at[1, way, c],
            bulk_recv.at[1, way, c],
            way,
        )

    def part_copy(c, way):
        return remote(
            part_out.at[way, c],
            part_in.at[way, c],
            stat_send.at[0, way, c],
            stat_recv.at[0, way, c],
            way,
        )

    def stat_copy(c, way):
        return remote(
            stat_out.at[c],
            stat_in.at[way, c],
            stat_send.at[1, way, c],
            stat_recv.at[1, way, c],
            way,
        )

    def dq_copy(c, way):
        return remote(
            dq_out.at[way, :, columns(c)],
            dq_in.at[way, :, columns(c)],
            dq_send.at[way, c],
            dq_recv.at[way, c],
            way,
        )

    def launch(copies, c):
        for way in (0, 1):

            @pl.when(edges[way])
            def _():
                for copy in copies:
                    copy(c, way).start()

    def arrive(copies, c):
        for way in (0, 1):

            @pl.when(sources[way])
            def _():
                for copy in copies:
                    copy(c, way).wait_recv()

    def sent(copies, c):
        for way in (0, 1):

            @pl.when(edges[way])
            def _():
                for copy in copies:
                    copy(c, way).wait_send()

    if fused:
        pl.semaphore_wait(barrier, dp + seq - 2)
    else:
        for side in (0, 1):

            @pl.when(sources[side])
            def _():
                pl.semaphore_wait(barrier, 1)

    for c in range(LEAD):
        launch((upstream_copy,), c)

    load_tokens.wait()
    for load in load_small:
        load.wait()
    low = dot_nt(tokens_ref[...], down_ref[...]).astype(BF16)
    load_frozen.wait()
    query_gain = query_gain_ref[...]
    key_gain = key_gain_ref[...]

    def normed(raw):
        inverse = lax.rsqrt(jnp.mean(raw * raw, axis=-1, keepdims=True) + EPSILON)
        return raw * inverse, inverse

    def project(part, c):
        cut = pl.ds(part * width + bounds[c][0] * head_dim, bounds[c][1] * head_dim)
        return frozen_ref[:, cut].astype(F32) + dot_nn(low, up_ref[:, cut])

    def project_heads(part, c, gain, target):
        raw = project(part, c)
        raw_ref[part, :, columns(c)] = raw
        for i in range(bounds[c][1]):
            h = bounds[c][0] + i
            one = raw[:, i * head_dim : (i + 1) * head_dim]
            target(h, (normed(one)[0] * gain).astype(BF16))

    def put_query(h, value):
        query_all[1, :, pl.ds(h * head_dim, head_dim)] = value

    def put_key(h, value):
        key_own[:, pl.ds(h * head_dim, head_dim)] = value

    for c in range(LEAD):
        project_heads(0, c, query_gain, put_query)
        launch((query_copy,), c)

    def project_bank(c):
        project_heads(1, c, key_gain, put_key)
        value_own[:, columns(c)] = project(2, c).astype(BF16)

    project_bank(0)
    load_upstream.wait()
    low_t = dot_nt(down_ref[...], tokens_ref[...]).astype(BF16)

    def spread(below, own, above):
        return jnp.concatenate([below, own, above], axis=1)

    def head_cut(h):
        return pl.ds(h * head_dim, head_dim)

    def stage_scores(c):
        head, count = bounds[c]
        for i in range(count):
            h = head + i
            queries = query_all[:, :, head_cut(h)].reshape(3 * rows, head_dim)
            upstream = upstream_all[:, :, head_cut(h)].reshape(3 * rows, head_dim)
            keep_below = mask_ref[jnp.maximum(me - 1, 0), 1, h].astype(F32)
            keep_above = mask_ref[jnp.minimum(me + 1, seq - 1), 0, h].astype(F32)
            keep_below = keep_below * has_below.astype(F32)
            keep_above = keep_above * has_above.astype(F32)
            keep = spread(
                jnp.full((1, rows), keep_below, F32),
                jnp.ones((1, rows), F32),
                jnp.full((1, rows), keep_above, F32),
            )
            scores = dot_nt(key_own[:, head_cut(h)], queries) * scale
            grown = jnp.exp(scores) * keep
            product = dot_nt(value_own[:, head_cut(h)], upstream)
            exp_all[h] = grown
            product_all[h] = product
            total = jnp.sum(grown, axis=0, keepdims=True)
            moment = jnp.sum(grown * product, axis=0, keepdims=True)
            for row, line in ((i, total), (4 + i, moment)):
                part_out[1, c, pl.ds(row, 1), :] = line[:, :rows]
                part_own[c, pl.ds(row, 1), :] = line[:, rows : 2 * rows]
                part_out[0, c, pl.ds(row, 1), :] = line[:, 2 * rows :]

    def stage_stats(c):
        whole = part_own[c] + part_in[0, c] + part_in[1, c]
        count = bounds[c][1]
        inverse = 1.0 / whole[:count]
        delta = whole[4 : 4 + count] * inverse
        stat_out[c, pl.ds(0, count), :] = inverse
        stat_out[c, pl.ds(4, count), :] = delta

    def norm_grad(raw, gain, upstream):
        unit, inverse = normed(raw)
        scaled = upstream * gain
        return inverse * (scaled - unit * jnp.mean(scaled * unit, axis=-1, keepdims=True))

    def absorb(part, c):
        cut = pl.ds(part * width + bounds[c][0] * head_dim, bounds[c][1] * head_dim)
        grad = grad_ref[:, cut]
        term_up[:, cut] = dot_nn(low_t, grad)
        return dot_nt(up_ref[:, cut], grad)

    def stage_grads(c):
        head, count = bounds[c]
        held = []
        for i in range(count):
            h = head + i
            inverse, delta = (
                spread(
                    *(
                        ref[c, pl.ds(row, 1), :]
                        for ref in (stat_in.at[0], stat_out, stat_in.at[1])
                    )
                )
                for row in (i, 4 + i)
            )
            weights = exp_all[h] * inverse
            grad_scores = (weights * (product_all[h] - delta)).astype(BF16)
            held.append((weights.astype(BF16), grad_scores))
            grad_query = dot_tn(grad_scores, key_own[:, head_cut(h)]) * scale
            dq_out[1, :, head_cut(h)] = grad_query[:rows].astype(BF16)
            dq_own[:, head_cut(h)] = grad_query[rows : 2 * rows]
            dq_out[0, :, head_cut(h)] = grad_query[2 * rows :].astype(BF16)
        launch((dq_copy,), c)
        for i in range(count):
            h = head + i
            weights_low, grad_scores = held[i]
            queries = query_all[:, :, head_cut(h)].reshape(3 * rows, head_dim)
            upstream = upstream_all[:, :, head_cut(h)].reshape(3 * rows, head_dim)
            grad_key = dot_nn(grad_scores, queries) * scale
            grad_value = dot_nn(weights_low, upstream)
            grad_ref[:, pl.ds(width + h * head_dim, head_dim)] = norm_grad(
                raw_ref[1, :, head_cut(h)], key_gain, grad_key
            ).astype(BF16)
            grad_ref[:, pl.ds(2 * width + h * head_dim, head_dim)] = grad_value.astype(BF16)
        low_grad[...] += absorb(1, c) + absorb(2, c)

    def stage_queries(c):
        head, count = bounds[c]
        for i in range(count):
            h = head + i
            grad_query = (
                dq_own[:, head_cut(h)]
                + dq_in[0, :, head_cut(h)].astype(F32)
                + dq_in[1, :, head_cut(h)].astype(F32)
            )
            grad_ref[:, head_cut(h)] = norm_grad(
                raw_ref[0, :, head_cut(h)], query_gain, grad_query
            ).astype(BF16)
        low_grad[...] += absorb(0, c)

    low_grad[...] = jnp.zeros(low_grad.shape, F32)
    for step in range(steps + 3):
        if step < steps:
            arrive((upstream_copy, query_copy), step)
            stage_scores(step)
            launch((part_copy,), step)
        if step + LEAD < steps:
            project_heads(0, step + LEAD, query_gain, put_query)
        if 0 <= step - 1 < steps:
            arrive((part_copy,), step - 1)
            stage_stats(step - 1)
            launch((stat_copy,), step - 1)
        if step + LEAD < steps:
            launch((upstream_copy, query_copy), step + LEAD)
        if step + 1 < steps:
            project_bank(step + 1)
        if 0 <= step - 2 < steps:
            arrive((stat_copy,), step - 2)
            stage_grads(step - 2)
        if 0 <= step - 3 < steps:
            arrive((dq_copy,), step - 3)
            stage_queries(step - 3)

    model_width = tokens_ref.shape[1]
    term_down = dot_nn(low_grad[...].astype(BF16), tokens_ref[...])
    norm_factor = float(dp * seq * rows) ** (-0.5)
    if not fused:
        lora_down_ref[...] = term_down
        lora_up_ref[...] = term_up[...]
    else:
        msg_own, msg_out, msg_in, line_out, line_in, dp_send, dp_recv, seq_send, seq_recv = reduce_refs
        down_share = model_width // dp
        up_share = 3 * width // dp
        packed = msg_own.shape[2]
        filler = 2 * packed - down_share - up_share
        for d in range(dp):
            pieces = [
                term_down[:, d * down_share : (d + 1) * down_share],
                term_up[:, d * up_share : (d + 1) * up_share],
            ]
            if filler:
                pieces.append(jnp.zeros((pieces[0].shape[0], filler), F32))
            line = jnp.concatenate(pieces, axis=1)
            line = jnp.concatenate([line[:, :packed], line[:, packed:]], axis=0)
            msg_own[d] = line
            msg_out[d] = line.astype(BF16)

        def dp_copy(j):
            peer = lax.rem(dp_me + j, dp)
            return pltpu.make_async_remote_copy(
                src_ref=msg_out.at[peer],
                dst_ref=msg_in.at[j - 1],
                send_sem=dp_send.at[j - 1],
                recv_sem=dp_recv.at[j - 1],
                device_id={"dp": peer},
                device_id_type=mesh_id,
            )

        def seq_copy(j):
            peer = lax.rem(me + j, seq)
            return pltpu.make_async_remote_copy(
                src_ref=line_out,
                dst_ref=line_in.at[me],
                send_sem=seq_send.at[j - 1],
                recv_sem=seq_recv.at[j - 1],
                device_id={"seq": peer},
                device_id_type=mesh_id,
            )

        for j in range(1, dp):
            dp_copy(j).start()
        for c in range(steps):
            sent((upstream_copy, query_copy, part_copy, stat_copy, dq_copy), c)
        summed = msg_own[dp_me]
        for j in range(1, dp):
            dp_copy(j).wait_recv()
            summed = summed + msg_in[j - 1].astype(F32)
        line_out[...] = summed.astype(BF16)
        line_in[me] = summed.astype(BF16)
        for j in range(1, seq):
            seq_copy(j).start()
        for j in range(1, dp):
            dp_copy(j).wait_send()
        for j in range(1, seq):
            seq_copy(j).wait_recv()
        result = line_in[0].astype(F32)
        for j in range(1, seq):
            result = result + line_in[j].astype(F32)
        result = result * norm_factor
        half = result.shape[0] // 2
        line = jnp.concatenate([result[:half], result[half:]], axis=1)
        lora_down_ref[...] = line[:, :down_share]
        lora_up_ref[...] = line[:, down_share : down_share + up_share]
        for j in range(1, seq):
            seq_copy(j).wait_send()
    if not fused:
        for c in range(steps):
            sent((upstream_copy, query_copy, part_copy, stat_copy, dq_copy), c)


def writer(*refs):
    sources, targets, sem = refs[:3], refs[3:6], refs[6]
    copies = [
        pltpu.make_async_copy(source, target, sem.at[i])
        for i, (source, target) in enumerate(zip(sources, targets))
    ]
    for copy in copies:
        copy.start()
    for copy in copies:
        copy.wait()


def write_out(*arrays):
    return pl.pallas_call(
        writer,
        out_shape=tuple(jax.ShapeDtypeStruct(a.shape, a.dtype) for a in arrays),
        in_specs=[pl.BlockSpec(memory_space=pltpu.VMEM)] * 3,
        out_specs=(pl.BlockSpec(memory_space=pltpu.HBM),) * 3,
        scratch_shapes=[pltpu.SemaphoreType.DMA((3,))],
        compiler_params=pltpu.CompilerParams(vmem_limit_bytes=4 * 1024 * 1024),
        name="write_out",
    )(*arrays)


def on_device(
    dp,
    seq,
    tokens,
    frozen_projection,
    output_gradient,
    adapter_down,
    adapter_up,
    query_norm_gain,
    key_norm_gain,
    neighbour_mask,
):
    clip_count, frames_dev, spatial, model_width = tokens.shape
    combined = frozen_projection.shape[-1]
    width = combined // 3
    head_dim = query_norm_gain.shape[0]
    heads = width // head_dim
    rank = adapter_up.shape[0]
    rows = clip_count * frames_dev * spatial
    assert clip_count == 1 and sum(CHUNKS) == heads
    steps = len(CHUNKS)
    down_share = model_width // dp
    up_share = combined // dp
    fused = dp <= 8 and seq <= 4 and down_share % 128 == 0
    mask_shape = (neighbour_mask.shape[0], 2, heads)
    vmem = pl.BlockSpec(memory_space=pltpu.VMEM)
    distant = pl.BlockSpec(memory_space=pltpu.HBM)
    dma = pltpu.SemaphoreType.DMA
    scratch = [
        pltpu.VMEM((rows, model_width), BF16),
        pltpu.VMEM((rows, combined), BF16),
        pltpu.VMEM((rank, model_width), BF16),
        pltpu.VMEM((rank, combined), BF16),
        pltpu.VMEM((1, head_dim), F32),
        pltpu.VMEM((1, head_dim), F32),
        pltpu.SMEM(mask_shape, jnp.int32),
        dma((8,)),
        pltpu.VMEM((3, rows, width), BF16),
        pltpu.VMEM((3, rows, width), BF16),
        pltpu.VMEM((rows, width), BF16),
        pltpu.VMEM((rows, width), BF16),
        pltpu.VMEM((2, rows, width), F32),
        pltpu.VMEM((heads, rows, 3 * rows), F32),
        pltpu.VMEM((heads, rows, 3 * rows), F32),
        pltpu.VMEM((2, steps, 8, rows), F32),
        pltpu.VMEM((2, steps, 8, rows), F32),
        pltpu.VMEM((steps, 8, rows), F32),
        pltpu.VMEM((steps, 8, rows), F32),
        pltpu.VMEM((2, steps, 8, rows), F32),
        pltpu.VMEM((2, rows, width), BF16),
        pltpu.VMEM((2, rows, width), BF16),
        pltpu.VMEM((rows, width), F32),
        pltpu.VMEM((rank, combined), F32),
        pltpu.VMEM((rank, rows), F32),
        dma((2, 2, steps)),
        dma((2, 2, steps)),
        dma((2, 2, steps)),
        dma((2, 2, steps)),
        dma((2, steps)),
        dma((2, steps)),
    ]
    if fused:
        packed = -(-(down_share + up_share) // 256) * 128
        scratch += [
            pltpu.VMEM((dp, 2 * rank, packed), F32),
            pltpu.VMEM((dp, 2 * rank, packed), BF16),
            pltpu.VMEM((dp - 1, 2 * rank, packed), BF16),
            pltpu.VMEM((2 * rank, packed), BF16),
            pltpu.VMEM((seq, 2 * rank, packed), BF16),
            dma((dp - 1,)),
            dma((dp - 1,)),
            dma((seq - 1,)),
            dma((seq - 1,)),
        ]
        lora_shapes = ((rank, down_share), (rank, up_share))
    else:
        lora_shapes = ((rank, model_width), (rank, combined))
    geometry = (rows, width, head_dim, dp, seq, fused)
    grad, lora_down, lora_up = pl.pallas_call(
        functools.partial(kernel, geometry),
        out_shape=(
            jax.ShapeDtypeStruct((rows, combined), BF16),
            jax.ShapeDtypeStruct(lora_shapes[0], F32),
            jax.ShapeDtypeStruct(lora_shapes[1], F32),
        ),
        in_specs=[distant] * 8,
        out_specs=(vmem, vmem, vmem),
        scratch_shapes=scratch,
        compiler_params=pltpu.CompilerParams(
            collective_id=0, has_side_effects=True, vmem_limit_bytes=48 * 1024 * 1024
        ),
        name="tile_attention",
    )(
        *(
            pltpu.with_memory_space_constraint(array, pltpu.HBM)
            for array in (
                tokens.reshape(rows, model_width),
                frozen_projection.reshape(rows, combined),
                output_gradient.reshape(rows, width),
                adapter_down.T,
                adapter_up,
                query_norm_gain.reshape(1, head_dim),
                key_norm_gain.reshape(1, head_dim),
                neighbour_mask.transpose(0, 2, 1),
            )
        )
    )
    if fused:
        grad, lora_down, lora_up = write_out(grad, lora_down, lora_up)
    grad = grad.reshape(frozen_projection.shape)
    if fused:
        return grad, lora_down.T, lora_up
    norm_factor = float(dp * seq * rows) ** (-0.5)
    whole_down, whole_up = lax.psum((lora_down, lora_up), ("dp", "seq"))
    dp_index = lax.axis_index("dp")
    mine_down = lax.dynamic_slice_in_dim(whole_down, dp_index * down_share, down_share, 1)
    mine_up = lax.dynamic_slice_in_dim(whole_up, dp_index * up_share, up_share, 1)
    return grad, mine_down.T * norm_factor, mine_up * norm_factor


def solution(mesh):
    dp, seq = mesh.shape["dp"], mesh.shape["seq"]
    return jax.shard_map(
        functools.partial(on_device, dp, seq),
        mesh=mesh,
        in_specs=(
            P("dp", "seq", None, None),
            P("dp", "seq", None, None),
            P("dp", "seq", None, None),
            P(),
            P(),
            P(),
            P(),
            P(),
        ),
        out_specs=(P("dp", "seq", None, None), P("dp", None), P(None, "dp")),
        check_vma=False,
    )
```

```python
import functools

import jax
import jax.numpy as jnp
from jax import lax
from jax.experimental import pallas as pl
from jax.experimental.pallas import tpu as pltpu
from jax.sharding import PartitionSpec as P

EPSILON = 1e-06
CHUNKS = (3, 4, 3, 2)
LEAD = 2
LAGS = (1, 2, 3)
F32 = jnp.float32
BF16 = jnp.bfloat16


def dot_nt(a, b):
    return lax.dot_general(a, b, (((1,), (1,)), ((), ())), preferred_element_type=F32)


def dot_nn(a, b):
    return lax.dot_general(a, b, (((1,), (0,)), ((), ())), preferred_element_type=F32)


def dot_tn(a, b):
    return lax.dot_general(a, b, (((0,), (0,)), ((), ())), preferred_element_type=F32)


def kernel(
    geometry,
    tokens_hbm,
    frozen_hbm,
    upstream_hbm,
    down_hbm,
    up_hbm,
    query_gain_hbm,
    key_gain_hbm,
    mask_hbm,
    grad_ref,
    lora_down_ref,
    lora_up_ref,
    tokens_ref,
    frozen_ref,
    down_ref,
    up_ref,
    query_gain_ref,
    key_gain_ref,
    mask_ref,
    load_sem,
    query_all,
    upstream_all,
    key_own,
    value_own,
    raw_ref,
    exp_all,
    product_all,
    part_out,
    part_in,
    part_own,
    stat_out,
    stat_in,
    dq_out,
    dq_in,
    dq_own,
    term_up,
    low_grad,
    bulk_send,
    bulk_recv,
    stat_send,
    stat_recv,
    dq_send,
    dq_recv,
    *reduce_refs,
):
    rows, width, head_dim, dp, seq, fused = geometry
    scale = head_dim ** (-0.5)
    heads = width // head_dim
    me = lax.axis_index("seq")
    has_below = me > 0
    has_above = me < seq - 1
    edges = (has_above, has_below)
    sources = (has_below, has_above)
    targets = ({"seq": me + 1}, {"seq": me - 1})
    mesh_id = pl.DeviceIdType.MESH
    barrier = pltpu.get_barrier_semaphore()
    if fused:
        dp_me = lax.axis_index("dp")
        for j in range(1, dp):
            pl.semaphore_signal(
                barrier, inc=1, device_id={"dp": lax.rem(dp_me + j, dp)}, device_id_type=mesh_id
            )
        for j in range(1, seq):
            pl.semaphore_signal(
                barrier, inc=1, device_id={"seq": lax.rem(me + j, seq)}, device_id_type=mesh_id
            )
    else:
        for way in (0, 1):

            @pl.when(edges[way])
            def _():
                pl.semaphore_signal(
                    barrier, inc=1, device_id=targets[way], device_id_type=mesh_id
                )

    load_tokens = pltpu.make_async_copy(tokens_hbm, tokens_ref, load_sem.at[0])
    load_frozen = pltpu.make_async_copy(frozen_hbm, frozen_ref, load_sem.at[1])
    load_upstream = [
        pltpu.make_async_copy(
            upstream_hbm.at[:, pl.ds(h * head_dim, head_dim)], upstream_all.at[1, h], load_sem.at[7 + h]
        )
        for h in range(heads)
    ]
    load_small = [
        pltpu.make_async_copy(source, target, load_sem.at[2 + i])
        for i, (source, target) in enumerate(
            (
                (down_hbm, down_ref),
                (up_hbm, up_ref),
                (query_gain_hbm, query_gain_ref),
                (key_gain_hbm, key_gain_ref),
                (mask_hbm, mask_ref),
            )
        )
    ]
    for load in load_upstream:
        load.start()
    load_tokens.start()
    for load in load_small:
        load.start()
    load_frozen.start()

    for side in (0, 1):

        @pl.when(jnp.logical_not(sources[side]))
        def _():
            query_all[2 * side] = jnp.zeros((heads, rows, head_dim), BF16)
            upstream_all[2 * side] = jnp.zeros((heads, rows, head_dim), BF16)
            part_in[side] = jnp.zeros(part_in.shape[1:], F32)
            stat_in[side] = jnp.zeros(stat_in.shape[1:], F32)
            dq_in[side] = jnp.zeros((heads, rows, head_dim), BF16)

    part_out[...] = jnp.zeros(part_out.shape, F32)
    part_own[...] = jnp.zeros(part_own.shape, F32)
    stat_out[...] = jnp.zeros(stat_out.shape, F32)

    bounds = []
    first = 0
    for count in CHUNKS:
        bounds.append((first, count))
        first += count
    steps = len(bounds)

    def columns(c):
        return pl.ds(bounds[c][0] * head_dim, bounds[c][1] * head_dim)

    def members(c):
        return pl.ds(*bounds[c])

    def remote(source, target, send, recv, way):
        return pltpu.make_async_remote_copy(
            src_ref=source,
            dst_ref=target,
            send_sem=send,
            recv_sem=recv,
            device_id=targets[way],
            device_id_type=mesh_id,
        )

    def query_copy(c, way):
        return remote(
            query_all.at[1, members(c)],
            query_all.at[2 * way, members(c)],
            bulk_send.at[0, way, c],
            bulk_recv.at[0, way, c],
            way,
        )

    def upstream_copy(c, way):
        return remote(
            upstream_all.at[1, members(c)],
            upstream_all.at[2 * way, members(c)],
            bulk_send.at[1, way, c],
            bulk_recv.at[1, way, c],
            way,
        )

    def part_copy(c, way):
        return remote(
            part_out.at[way, c],
            part_in.at[way, c],
            stat_send.at[0, way, c],
            stat_recv.at[0, way, c],
            way,
        )

    def stat_copy(c, way):
        return remote(
            stat_out.at[c],
            stat_in.at[way, c],
            stat_send.at[1, way, c],
            stat_recv.at[1, way, c],
            way,
        )

    def dq_copy(c, way):
        return remote(
            dq_out.at[way, members(c)],
            dq_in.at[way, members(c)],
            dq_send.at[way, c],
            dq_recv.at[way, c],
            way,
        )

    def launch(copies, c):
        for way in (0, 1):

            @pl.when(edges[way])
            def _():
                for copy in copies:
                    copy(c, way).start()

    def arrive(copies, c):
        for way in (0, 1):

            @pl.when(sources[way])
            def _():
                for copy in copies:
                    copy(c, way).wait_recv()

    def sent(copies, c):
        for way in (0, 1):

            @pl.when(edges[way])
            def _():
                for copy in copies:
                    copy(c, way).wait_send()

    if fused:
        pl.semaphore_wait(barrier, dp + seq - 2)
    else:
        for side in (0, 1):

            @pl.when(sources[side])
            def _():
                pl.semaphore_wait(barrier, 1)

    for load in load_upstream:
        load.wait()
    launch((upstream_copy,), 0)

    load_tokens.wait()
    for load in load_small:
        load.wait()
    low = dot_nt(tokens_ref[...], down_ref[...]).astype(BF16)
    load_frozen.wait()
    query_gain = query_gain_ref[...]
    key_gain = key_gain_ref[...]

    def normed(raw):
        inverse = lax.rsqrt(jnp.mean(raw * raw, axis=-1, keepdims=True) + EPSILON)
        return raw * inverse, inverse

    def project(part, c):
        cut = pl.ds(part * width + bounds[c][0] * head_dim, bounds[c][1] * head_dim)
        return frozen_ref[:, cut].astype(F32) + dot_nn(low, up_ref[:, cut])

    def project_heads(part, c, gain, target):
        raw = project(part, c)
        raw_ref[part, :, columns(c)] = raw
        for i in range(bounds[c][1]):
            h = bounds[c][0] + i
            one = raw[:, i * head_dim : (i + 1) * head_dim]
            target(h, (normed(one)[0] * gain).astype(BF16))

    def put_query(h, value):
        query_all[1, h] = value

    def put_key(h, value):
        key_own[:, pl.ds(h * head_dim, head_dim)] = value

    for c in range(LEAD):
        project_heads(0, c, query_gain, put_query)
        launch((query_copy,), c)
        if c + 1 < LEAD:
            launch((upstream_copy,), c + 1)

    def project_bank(c):
        project_heads(1, c, key_gain, put_key)
        value_own[:, columns(c)] = project(2, c).astype(BF16)

    project_bank(0)
    low_t = dot_nt(down_ref[...], tokens_ref[...]).astype(BF16)

    def spread(below, own, above):
        return jnp.concatenate([below, own, above], axis=1)

    def head_cut(h):
        return pl.ds(h * head_dim, head_dim)

    def stage_scores(c):
        head, count = bounds[c]
        for i in range(count):
            h = head + i
            queries = query_all[:, h].reshape(3 * rows, head_dim)
            upstream = upstream_all[:, h].reshape(3 * rows, head_dim)
            keep_below = mask_ref[jnp.maximum(me - 1, 0), 1, h].astype(F32)
            keep_above = mask_ref[jnp.minimum(me + 1, seq - 1), 0, h].astype(F32)
            keep_below = keep_below * has_below.astype(F32)
            keep_above = keep_above * has_above.astype(F32)
            keep = spread(
                jnp.full((1, rows), keep_below, F32),
                jnp.ones((1, rows), F32),
                jnp.full((1, rows), keep_above, F32),
            )
            scores = dot_nt(key_own[:, head_cut(h)], queries) * scale
            grown = jnp.exp(scores) * keep
            product = dot_nt(value_own[:, head_cut(h)], upstream)
            exp_all[h] = grown
            product_all[h] = product
            total = jnp.sum(grown, axis=0, keepdims=True)
            moment = jnp.sum(grown * product, axis=0, keepdims=True)
            for row, line in ((i, total), (4 + i, moment)):
                part_out[1, c, pl.ds(row, 1), :] = line[:, :rows]
                part_own[c, pl.ds(row, 1), :] = line[:, rows : 2 * rows]
                part_out[0, c, pl.ds(row, 1), :] = line[:, 2 * rows :]

    def stage_stats(c):
        whole = part_own[c] + part_in[0, c] + part_in[1, c]
        count = bounds[c][1]
        inverse = 1.0 / whole[:count]
        delta = whole[4 : 4 + count] * inverse
        stat_out[c, pl.ds(0, count), :] = inverse
        stat_out[c, pl.ds(4, count), :] = delta

    def norm_grad(raw, gain, upstream):
        unit, inverse = normed(raw)
        scaled = upstream * gain
        return inverse * (scaled - unit * jnp.mean(scaled * unit, axis=-1, keepdims=True))

    def absorb(part, c):
        cut = pl.ds(part * width + bounds[c][0] * head_dim, bounds[c][1] * head_dim)
        grad = grad_ref[:, cut]
        term_up[:, cut] = dot_nn(low_t, grad)
        return dot_nt(up_ref[:, cut], grad)

    def stage_grads(c):
        head, count = bounds[c]
        held = []
        for i in range(count):
            h = head + i
            inverse, delta = (
                spread(
                    *(
                        ref[c, pl.ds(row, 1), :]
                        for ref in (stat_in.at[0], stat_out, stat_in.at[1])
                    )
                )
                for row in (i, 4 + i)
            )
            weights = exp_all[h] * inverse
            grad_scores = (weights * (product_all[h] - delta)).astype(BF16)
            held.append((weights.astype(BF16), grad_scores))
            grad_query = dot_tn(grad_scores, key_own[:, head_cut(h)]) * scale
            dq_out[1, h] = grad_query[:rows].astype(BF16)
            dq_own[:, head_cut(h)] = grad_query[rows : 2 * rows]
            dq_out[0, h] = grad_query[2 * rows :].astype(BF16)
        launch((dq_copy,), c)
        for i in range(count):
            h = head + i
            weights_low, grad_scores = held[i]
            queries = query_all[:, h].reshape(3 * rows, head_dim)
            upstream = upstream_all[:, h].reshape(3 * rows, head_dim)
            grad_key = dot_nn(grad_scores, queries) * scale
            grad_value = dot_nn(weights_low, upstream)
            grad_ref[:, pl.ds(width + h * head_dim, head_dim)] = norm_grad(
                raw_ref[1, :, head_cut(h)], key_gain, grad_key
            ).astype(BF16)
            grad_ref[:, pl.ds(2 * width + h * head_dim, head_dim)] = grad_value.astype(BF16)
        low_grad[...] += absorb(1, c) + absorb(2, c)

    def stage_queries(c):
        head, count = bounds[c]
        for i in range(count):
            h = head + i
            grad_query = (
                dq_own[:, head_cut(h)]
                + dq_in[0, h].astype(F32)
                + dq_in[1, h].astype(F32)
            )
            grad_ref[:, head_cut(h)] = norm_grad(
                raw_ref[0, :, head_cut(h)], query_gain, grad_query
            ).astype(BF16)
        low_grad[...] += absorb(0, c)

    low_grad[...] = jnp.zeros(low_grad.shape, F32)
    for step in range(steps + LAGS[2]):
        if step < steps:
            arrive((upstream_copy, query_copy), step)
            stage_scores(step)
            launch((part_copy,), step)
        if step + LEAD < steps:
            project_heads(0, step + LEAD, query_gain, put_query)
        past = step - LAGS[0]
        if 0 <= past < steps:
            arrive((part_copy,), past)
            stage_stats(past)
            launch((stat_copy,), past)
        if step + LEAD < steps:
            launch((upstream_copy, query_copy), step + LEAD)
        if step + 1 < steps:
            project_bank(step + 1)
        past = step - LAGS[1]
        if 0 <= past < steps:
            arrive((stat_copy,), past)
            stage_grads(past)
        past = step - LAGS[2]
        if 0 <= past < steps:
            arrive((dq_copy,), past)
            stage_queries(past)

    model_width = tokens_ref.shape[1]
    term_down = dot_nn(low_grad[...].astype(BF16), tokens_ref[...])
    norm_factor = float(dp * seq * rows) ** (-0.5)
    if not fused:
        lora_down_ref[...] = term_down
        lora_up_ref[...] = term_up[...]
    else:
        msg_own, msg_out, msg_in, line_out, line_in, dp_send, dp_recv, seq_send, seq_recv = reduce_refs
        down_share = model_width // dp
        up_share = 3 * width // dp
        packed = msg_own.shape[2]
        filler = 2 * packed - down_share - up_share
        for d in range(dp):
            pieces = [
                term_down[:, d * down_share : (d + 1) * down_share],
                term_up[:, d * up_share : (d + 1) * up_share],
            ]
            if filler:
                pieces.append(jnp.zeros((pieces[0].shape[0], filler), F32))
            line = jnp.concatenate(pieces, axis=1)
            line = jnp.concatenate([line[:, :packed], line[:, packed:]], axis=0)
            msg_own[d] = line
            msg_out[d] = line.astype(BF16)

        def dp_copy(j):
            peer = lax.rem(dp_me + j, dp)
            return pltpu.make_async_remote_copy(
                src_ref=msg_out.at[peer],
                dst_ref=msg_in.at[j - 1],
                send_sem=dp_send.at[j - 1],
                recv_sem=dp_recv.at[j - 1],
                device_id={"dp": peer},
                device_id_type=mesh_id,
            )

        def seq_copy(j):
            peer = lax.rem(me + j, seq)
            return pltpu.make_async_remote_copy(
                src_ref=line_out,
                dst_ref=line_in.at[me],
                send_sem=seq_send.at[j - 1],
                recv_sem=seq_recv.at[j - 1],
                device_id={"seq": peer},
                device_id_type=mesh_id,
            )

        for j in range(1, dp):
            dp_copy(j).start()
        for c in range(steps):
            sent((upstream_copy, query_copy, part_copy, stat_copy, dq_copy), c)
        summed = msg_own[dp_me]
        for j in range(1, dp):
            dp_copy(j).wait_recv()
            summed = summed + msg_in[j - 1].astype(F32)
        line_out[...] = summed.astype(BF16)
        line_in[me] = summed.astype(BF16)
        for j in range(1, seq):
            seq_copy(j).start()
        for j in range(1, dp):
            dp_copy(j).wait_send()
        for j in range(1, seq):
            seq_copy(j).wait_recv()
        result = line_in[0].astype(F32)
        for j in range(1, seq):
            result = result + line_in[j].astype(F32)
        result = result * norm_factor
        half = result.shape[0] // 2
        line = jnp.concatenate([result[:half], result[half:]], axis=1)
        lora_down_ref[...] = line[:, :down_share]
        lora_up_ref[...] = line[:, down_share : down_share + up_share]
        for j in range(1, seq):
            seq_copy(j).wait_send()
    if not fused:
        for c in range(steps):
            sent((upstream_copy, query_copy, part_copy, stat_copy, dq_copy), c)


def writer(*refs):
    sources, targets, sem = refs[:3], refs[3:6], refs[6]
    copies = [
        pltpu.make_async_copy(source, target, sem.at[i])
        for i, (source, target) in enumerate(zip(sources, targets))
    ]
    for copy in copies:
        copy.start()
    for copy in copies:
        copy.wait()


def write_out(*arrays):
    return pl.pallas_call(
        writer,
        out_shape=tuple(jax.ShapeDtypeStruct(a.shape, a.dtype) for a in arrays),
        in_specs=[pl.BlockSpec(memory_space=pltpu.VMEM)] * 3,
        out_specs=(pl.BlockSpec(memory_space=pltpu.HBM),) * 3,
        scratch_shapes=[pltpu.SemaphoreType.DMA((3,))],
        compiler_params=pltpu.CompilerParams(vmem_limit_bytes=4 * 1024 * 1024),
        name="write_out",
    )(*arrays)


def on_device(
    dp,
    seq,
    tokens,
    frozen_projection,
    output_gradient,
    adapter_down,
    adapter_up,
    query_norm_gain,
    key_norm_gain,
    neighbour_mask,
):
    clip_count, frames_dev, spatial, model_width = tokens.shape
    combined = frozen_projection.shape[-1]
    width = combined // 3
    head_dim = query_norm_gain.shape[0]
    heads = width // head_dim
    rank = adapter_up.shape[0]
    rows = clip_count * frames_dev * spatial
    assert clip_count == 1 and sum(CHUNKS) == heads
    steps = len(CHUNKS)
    down_share = model_width // dp
    up_share = combined // dp
    fused = dp <= 8 and seq <= 4 and down_share % 128 == 0
    mask_shape = (neighbour_mask.shape[0], 2, heads)
    vmem = pl.BlockSpec(memory_space=pltpu.VMEM)
    distant = pl.BlockSpec(memory_space=pltpu.HBM)
    dma = pltpu.SemaphoreType.DMA
    scratch = [
        pltpu.VMEM((rows, model_width), BF16),
        pltpu.VMEM((rows, combined), BF16),
        pltpu.VMEM((rank, model_width), BF16),
        pltpu.VMEM((rank, combined), BF16),
        pltpu.VMEM((1, head_dim), F32),
        pltpu.VMEM((1, head_dim), F32),
        pltpu.SMEM(mask_shape, jnp.int32),
        dma((7 + heads,)),
        pltpu.VMEM((3, heads, rows, head_dim), BF16),
        pltpu.VMEM((3, heads, rows, head_dim), BF16),
        pltpu.VMEM((rows, width), BF16),
        pltpu.VMEM((rows, width), BF16),
        pltpu.VMEM((2, rows, width), F32),
        pltpu.VMEM((heads, rows, 3 * rows), F32),
        pltpu.VMEM((heads, rows, 3 * rows), F32),
        pltpu.VMEM((2, steps, 8, rows), F32),
        pltpu.VMEM((2, steps, 8, rows), F32),
        pltpu.VMEM((steps, 8, rows), F32),
        pltpu.VMEM((steps, 8, rows), F32),
        pltpu.VMEM((2, steps, 8, rows), F32),
        pltpu.VMEM((2, heads, rows, head_dim), BF16),
        pltpu.VMEM((2, heads, rows, head_dim), BF16),
        pltpu.VMEM((rows, width), F32),
        pltpu.VMEM((rank, combined), F32),
        pltpu.VMEM((rank, rows), F32),
        dma((2, 2, steps)),
        dma((2, 2, steps)),
        dma((2, 2, steps)),
        dma((2, 2, steps)),
        dma((2, steps)),
        dma((2, steps)),
    ]
    if fused:
        packed = -(-(down_share + up_share) // 256) * 128
        scratch += [
            pltpu.VMEM((dp, 2 * rank, packed), F32),
            pltpu.VMEM((dp, 2 * rank, packed), BF16),
            pltpu.VMEM((dp - 1, 2 * rank, packed), BF16),
            pltpu.VMEM((2 * rank, packed), BF16),
            pltpu.VMEM((seq, 2 * rank, packed), BF16),
            dma((dp - 1,)),
            dma((dp - 1,)),
            dma((seq - 1,)),
            dma((seq - 1,)),
        ]
        lora_shapes = ((rank, down_share), (rank, up_share))
    else:
        lora_shapes = ((rank, model_width), (rank, combined))
    geometry = (rows, width, head_dim, dp, seq, fused)
    grad, lora_down, lora_up = pl.pallas_call(
        functools.partial(kernel, geometry),
        out_shape=(
            jax.ShapeDtypeStruct((rows, combined), BF16),
            jax.ShapeDtypeStruct(lora_shapes[0], F32),
            jax.ShapeDtypeStruct(lora_shapes[1], F32),
        ),
        in_specs=[distant] * 8,
        out_specs=(vmem, vmem, vmem),
        scratch_shapes=scratch,
        compiler_params=pltpu.CompilerParams(
            collective_id=0, has_side_effects=True, vmem_limit_bytes=48 * 1024 * 1024
        ),
        name="tile_attention",
    )(
        *(
            pltpu.with_memory_space_constraint(array, pltpu.HBM)
            for array in (
                tokens.reshape(rows, model_width),
                frozen_projection.reshape(rows, combined),
                output_gradient.reshape(rows, width),
                adapter_down.T,
                adapter_up,
                query_norm_gain.reshape(1, head_dim),
                key_norm_gain.reshape(1, head_dim),
                neighbour_mask.transpose(0, 2, 1),
            )
        )
    )
    if fused:
        grad, lora_down, lora_up = write_out(grad, lora_down, lora_up)
    grad = grad.reshape(frozen_projection.shape)
    if fused:
        return grad, lora_down.T, lora_up
    norm_factor = float(dp * seq * rows) ** (-0.5)
    whole_down, whole_up = lax.psum((lora_down, lora_up), ("dp", "seq"))
    dp_index = lax.axis_index("dp")
    mine_down = lax.dynamic_slice_in_dim(whole_down, dp_index * down_share, down_share, 1)
    mine_up = lax.dynamic_slice_in_dim(whole_up, dp_index * up_share, up_share, 1)
    return grad, mine_down.T * norm_factor, mine_up * norm_factor


def solution(mesh):
    dp, seq = mesh.shape["dp"], mesh.shape["seq"]
    return jax.shard_map(
        functools.partial(on_device, dp, seq),
        mesh=mesh,
        in_specs=(
            P("dp", "seq", None, None),
            P("dp", "seq", None, None),
            P("dp", "seq", None, None),
            P(),
            P(),
            P(),
            P(),
            P(),
        ),
        out_specs=(P("dp", "seq", None, None), P("dp", None), P(None, "dp")),
        check_vma=False,
    )
```
